32 devices in a mesh: groups: 2 (over y), role: 4 (over x, core), tp: 4 (over z).
Axes of the slice: x: 2, y: 2, z: 4, core: 2. Of those that a mesh axis runs over, the one named last changes fastest.
Arguments:
- x_teacher: bfloat16 [512, 8192], P('groups', 'tp'), parts along dimension 0, may hold values from -6 to 6
- x_student: bfloat16 [512, 4096], P('groups', 'role'), parts along dimension 0, may hold values from -6 to 6
- t_gate: bfloat16 [8192, 14336], P('tp', 'role'), may hold values from -0.0625 to 0.0625
- t_up: bfloat16 [8192, 14336], P('tp', 'role'), may hold values from -0.0625 to 0.0625
- t_down: bfloat16 [14336, 8192], P('role', 'tp'), may hold values from -0.046875 to 0.046875
- s_gate: bfloat16 [4096, 8192], P('role', 'tp'), may hold values from -0.09375 to 0.09375
- s_up: bfloat16 [4096, 8192], P('role', 'tp'), may hold values from -0.09375 to 0.09375
- s_down: bfloat16 [8192, 4096], P('tp', 'role'), may hold values from -0.0625 to 0.0625
- align: bfloat16 [4096, 8192], P('role', 'tp'), may hold values from -0.09375 to 0.09375
Outputs:
- grad_s_gate: bfloat16 [8192, 8192], P(('groups', 'role'), 'tp'), parts along dimension 0
- grad_s_up: bfloat16 [8192, 8192], P(('groups', 'role'), 'tp'), parts along dimension 0
- grad_s_down: bfloat16 [16384, 4096], P(('groups', 'tp'), 'role'), parts along dimension 0
- grad_align: bfloat16 [8192, 8192], P(('groups', 'role'), 'tp'), parts along dimension 0
The draws below stay inside these ranges and needn't reach their ends.
There are 2 independent parts, one for each index of `groups`. The reference program is written for one: setup_inputs(seed, part) draws one part's arguments, and reference() takes and returns one part's arrays. A program takes and returns all parts, laid end to end along the dimension named above; an argument that names none is the same for every part. Nothing has to cross between parts.
All inputs are finite; a program needn't handle non-finite values.
Results may differ from the reference program's by a relative error of at most 0.009.
Values may be sent and summed in bfloat16 or wider, within the bound.
No kernel may reach another device: no remote copies, remote signals or barrier semaphores. Data moves between devices by JAX's collectives and lax.ppermute only.
A program may use at most 128 MiB of HBM per device.

```python
import jax
import jax.numpy as jnp
from jax import lax

DT = 8192
DS = 4096
FT = 14336
FS = 8192
TOK = 256


def strengthened(values, stream_key, source, target, blocks, factor):
    def block_of(position):
        return (jnp.arange(values.shape[position]) // (values.shape[position] // blocks)).reshape((-1,) + (1,) * (values.ndim - 1 - position))

    first = jax.random.permutation(stream_key, blocks)[block_of(target)]
    other_side = (block_of(target) + blocks // 2) % blocks
    return jnp.where((block_of(source) == first) | (block_of(source) == other_side), factor * values, values)


def steps_of(stream_key, dims, split, low, high):
    gain = 1.0
    for axis_at, parts in split:
        draws = jax.random.uniform(jax.random.fold_in(jax.random.fold_in(stream_key, 6), axis_at), (parts,), jnp.float32, low / len(split), high / len(split))
        gain = gain * jnp.repeat(jnp.exp(draws), dims[axis_at] // parts).reshape((-1,) + (1,) * (len(dims) - 1 - axis_at))
    return gain


def gaussian(key, dims, scale, bound, shards=(), dtype=jnp.bfloat16):
    drawn = jax.random.normal(key, dims, jnp.float32) * scale
    if len(shards) > 0:
        drawn = steps_of(key, dims, shards, -0.22, 0.18) * drawn
    return jnp.clip(drawn, min=-bound, max=bound).astype(dtype)


def bell_draw_with(key, shape, spread, limit, shards, heavy, dtype=jnp.bfloat16):
    result = spread * jax.random.normal(key, shape, jnp.float32)
    if shards:
        result = result * steps_of(key, shape, shards, -0.22, 0.18)
    return jnp.clip(strengthened(result, jax.random.fold_in(key, 3), *heavy), -limit, limit).astype(dtype)


def setup_inputs(seed: int = 0, part: int = 0) -> dict:
    seeds = jax.random.split(jax.random.key(seed), 10)
    part_splits = jax.random.split(jax.random.fold_in(seeds[9], part), 10)
    x_teacher = bell_draw_with(part_splits[0], (TOK, DT), 1.0, 6.0, ((1, 4),), (1, 0, 4, 2.0))
    x_student = gaussian(part_splits[1], (TOK, DS), 1.0, 6.0, ((1, 4),))
    t_gate = gaussian(seeds[2], (DT, FT), DT ** -0.5, 0.0625, ((0, 4), (1, 4)))
    t_up = gaussian(seeds[3], (DT, FT), DT ** -0.5, 0.0625, ((0, 4), (1, 4)))
    t_down = gaussian(seeds[4], (FT, DT), FT ** -0.5, 0.046875, ((0, 4), (1, 4)))
    s_gate = gaussian(seeds[5], (DS, FS), DS ** -0.5, 0.09375, ((0, 4), (1, 4)))
    s_up = gaussian(seeds[6], (DS, FS), DS ** -0.5, 0.09375, ((0, 4), (1, 4)))
    s_down = gaussian(seeds[7], (FS, DS), FS ** -0.5, 0.0625, ((0, 4), (1, 4)))
    align = gaussian(seeds[8], (DS, DT), DS ** -0.5, 0.09375, ((0, 4), (1, 4)))
    return dict(x_teacher=x_teacher, x_student=x_student, t_gate=t_gate, t_up=t_up, t_down=t_down, s_gate=s_gate, s_up=s_up, s_down=s_down, align=align)


loss_scale = 16.0


def contract_rows(left, right):
    return lax.dot_general(left, right, (((0,), (0,)), ((), ())), preferred_element_type=jnp.float32)


def contract_cols(left, right):
    return lax.dot_general(left, right, (((1,), (1,)), ((), ())), preferred_element_type=jnp.float32)


def reference(x_teacher, x_student, t_gate, t_up, t_down, s_gate, s_up, s_down, align):
    teacher_gate = jnp.dot(x_teacher, t_gate, preferred_element_type=jnp.float32)
    teacher_up = jnp.dot(x_teacher, t_up, preferred_element_type=jnp.float32)
    teacher_hidden = (jax.nn.silu(teacher_gate) * teacher_up).astype(jnp.bfloat16)
    features = jnp.dot(teacher_hidden, t_down, preferred_element_type=jnp.float32)
    student_gate = jnp.dot(x_student, s_gate, preferred_element_type=jnp.float32)
    student_up = jnp.dot(x_student, s_up, preferred_element_type=jnp.float32)
    gate_sigmoid = jax.nn.sigmoid(student_gate)
    gate_active = student_gate * gate_sigmoid
    student_hidden = (gate_active * student_up).astype(jnp.bfloat16)
    student_out = jnp.dot(student_hidden, s_down, preferred_element_type=jnp.float32).astype(jnp.bfloat16)
    aligned = jnp.dot(student_out, align, preferred_element_type=jnp.float32)
    grad_aligned = ((aligned - features) * (2.0 * loss_scale / TOK)).astype(jnp.bfloat16)
    grad_align = contract_rows(student_out, grad_aligned).astype(jnp.bfloat16)
    grad_student_out = contract_cols(grad_aligned, align).astype(jnp.bfloat16)
    grad_s_down = contract_rows(student_hidden, grad_student_out).astype(jnp.bfloat16)
    grad_hidden = contract_cols(grad_student_out, s_down)
    slope = gate_sigmoid * (1.0 + student_gate * (1.0 - gate_sigmoid))
    grad_gate_pre = (grad_hidden * student_up * slope).astype(jnp.bfloat16)
    grad_up_pre = (grad_hidden * gate_active).astype(jnp.bfloat16)
    grad_s_gate = contract_rows(x_student, grad_gate_pre).astype(jnp.bfloat16)
    grad_s_up = contract_rows(x_student, grad_up_pre).astype(jnp.bfloat16)
    return (grad_s_gate, grad_s_up, grad_s_down, grad_align)
```

```python
import functools

import jax
import jax.numpy as jnp
from jax import lax
from jax.experimental import pallas as pl
from jax.experimental.pallas import tpu as pltpu
from jax.sharding import PartitionSpec as P

loss_scale = 16.0
f32 = jnp.float32
bf16 = jnp.bfloat16
MiB = 1 << 20


HBM = pl.BlockSpec(memory_space=pltpu.HBM)
VMEM = pl.BlockSpec(memory_space=pltpu.VMEM)
NN = (((1,), (0,)), ((), ()))
NT = (((1,), (1,)), ((), ()))


def parity(axis):
    return lax.rem(lax.axis_index(axis), 2)


def cost(flops, moved):
    return pl.CostEstimate(flops=flops, bytes_accessed=moved, transcendentals=0)


def nbytes(*arrays):
    return sum(a.size * a.dtype.itemsize for a in arrays)


def terms_body(jobs, pieces, x_ref, *refs):
    weights, refs = refs[: len(jobs[0][0])], refs[len(jobs[0][0]) :]
    outs, (x_buf, w_buf, x_sem, w_sem) = refs[: len(jobs)], refs[len(jobs) :]
    deep, width = w_buf.shape[2:]
    odd = parity("role")

    def x_copy(i):
        return pltpu.make_async_copy(
            x_ref.at[:, pl.ds(i * deep, deep)], x_buf.at[i], x_sem.at[i]
        )

    def w_copy(j, i):
        which, side_of = jobs[j][1:3]
        side = pl.multiple_of(side_of(odd) * width, 128)
        return pltpu.make_async_copy(
            weights[which].at[pl.ds(i * deep, deep), pl.ds(side, width)],
            w_buf.at[j, i],
            w_sem.at[j, i],
        )

    for j in range(len(jobs)):
        for i in range(pieces):
            if j == 0:
                x_copy(i).start()
            w_copy(j, i).start()
    for j in range(len(jobs)):
        total = None
        for i in range(pieces):
            if j == 0:
                x_copy(i).wait()
            w_copy(j, i).wait()
            term = jnp.dot(x_buf[i], w_buf[j, i], preferred_element_type=f32)
            total = term if total is None else total + term
        outs[j][...] = total.astype(outs[j].dtype)


def terms(x, weights, width, jobs):
    rows, depth = x.shape
    if width % 128:
        odd = parity("role")
        cut = [
            lax.dynamic_slice_in_dim(weights[w], side(odd) * width, width, 1)
            for w, side, _ in jobs
        ]
        return [
            jnp.dot(x, c, preferred_element_type=f32).astype(j[2])
            for c, j in zip(cut, jobs)
        ]
    pieces = 4 if depth % 1024 == 0 else 1
    deep = depth // pieces
    named = [(weights, *job) for job in jobs]
    outs = [jax.ShapeDtypeStruct((rows, width), j[2]) for j in jobs]
    return pl.pallas_call(
        functools.partial(terms_body, named, pieces),
        in_specs=[HBM] * (1 + len(weights)),
        out_specs=[VMEM] * len(jobs),
        out_shape=outs,
        scratch_shapes=[
            pltpu.VMEM((pieces, rows, deep), bf16),
            pltpu.VMEM((len(jobs), pieces, deep, width), bf16),
            pltpu.SemaphoreType.DMA((pieces,)),
            pltpu.SemaphoreType.DMA((len(jobs), pieces)),
        ],
        compiler_params=pltpu.CompilerParams(vmem_limit_bytes=20 * MiB),
        cost_estimate=cost(
            2 * len(jobs) * rows * depth * width,
            2 * len(jobs) * depth * width + nbytes(x, *outs),
        ),
    )(x, *weights)


def halves_body(axis, dims, left_ref, right_ref, keep_ref, give_ref):
    odd = parity(axis)
    width = keep_ref.shape[1]
    left = left_ref[...]
    for out, side in ((give_ref, 1 - odd), (keep_ref, odd)):
        cut = pl.ds(pl.multiple_of(side * width, 128), width)
        right = right_ref[:, cut] if dims == NN else right_ref[cut, :]
        term = lax.dot_general(left, right, dims, preferred_element_type=f32)
        out[...] = term.astype(out.dtype)


def halves(axis, dims, left, right):
    rows = left.shape[0]
    width = (right.shape[1] if dims == NN else right.shape[0]) // 2
    outs = [
        jax.ShapeDtypeStruct((rows, width), f32),
        jax.ShapeDtypeStruct((rows, width), bf16),
    ]
    return pl.pallas_call(
        functools.partial(halves_body, axis, dims),
        in_specs=[VMEM] * 2,
        out_specs=[VMEM] * 2,
        out_shape=outs,
        compiler_params=pltpu.CompilerParams(vmem_limit_bytes=16 * MiB),
        cost_estimate=cost(
            2 * left.shape[0] * right.size, nbytes(left, right, *outs)
        ),
    )(left, right)


def difference_body(stripes, hidden_ref, out_ref, down_ref, align_ref, keep_ref, give_ref):
    odd = parity("role")
    width = keep_ref.shape[1]
    tile = 256 if width % 256 == 0 else width
    depth = hidden_ref.shape[2]
    for result, side in ((give_ref, 1 - odd), (keep_ref, odd)):
        for first in range(0, width, tile):
            cut = pl.ds(pl.multiple_of(side * width + first, 128), tile)
            total = jnp.dot(out_ref[...], align_ref[:, cut], preferred_element_type=f32)
            for s in (0, 1):
                upward = 1 - odd if s == 0 else odd
                for q in range(stripes):
                    row = pl.multiple_of((upward * stripes + q) * depth, 64)
                    total -= jnp.dot(
                        hidden_ref[s * stripes + q],
                        down_ref[pl.ds(row, depth), cut],
                        preferred_element_type=f32,
                    )
            result[:, first : first + tile] = total.astype(result.dtype)


def difference_terms(stripes, hidden, out, down, align):
    rows, width = out.shape[0], down.shape[1] // 2
    outs = [
        jax.ShapeDtypeStruct((rows, width), f32),
        jax.ShapeDtypeStruct((rows, width), bf16),
    ]
    return pl.pallas_call(
        functools.partial(difference_body, stripes),
        in_specs=[VMEM] * 4,
        out_specs=[VMEM] * 2,
        out_shape=outs,
        compiler_params=pltpu.CompilerParams(vmem_limit_bytes=30 * MiB),
        cost_estimate=cost(
            2 * rows * (down.size + align.size),
            nbytes(hidden, out, down, align, *outs),
        ),
    )(hidden, out, down, align)


def turned_body(x_ref, o_ref):
    o_ref[...] = x_ref[...].T


def turned(x):
    return pl.pallas_call(
        turned_body,
        in_specs=[VMEM],
        out_specs=VMEM,
        out_shape=jax.ShapeDtypeStruct(x.shape[::-1], x.dtype),
        compiler_params=pltpu.CompilerParams(vmem_limit_bytes=8 * MiB),
        cost_estimate=cost(0, 2 * nbytes(x)),
    )(x)


def outer_body(left_ref, a_ref, b_ref, oa_ref, ob_ref):
    left = left_ref[...]
    oa_ref[...] = jnp.dot(left, a_ref[...], preferred_element_type=f32).astype(bf16)
    ob_ref[...] = jnp.dot(left, b_ref[...], preferred_element_type=f32).astype(bf16)


def outer_pair(left, a, b):
    rows, tokens = left.shape
    width = a.shape[1]
    block = 128 if rows % 128 == 0 else rows
    right = pl.BlockSpec((tokens, width), lambda j: (0, 0))
    result = pl.BlockSpec((block, width), lambda j: (j, 0))
    outs = [jax.ShapeDtypeStruct((rows, width), bf16)] * 2
    return pl.pallas_call(
        outer_body,
        grid=(rows // block,),
        in_specs=[pl.BlockSpec((block, tokens), lambda j: (j, 0)), right, right],
        out_specs=[result, result],
        out_shape=outs,
        compiler_params=pltpu.CompilerParams(vmem_limit_bytes=24 * MiB),
        cost_estimate=cost(4 * rows * tokens * width, nbytes(left, a, b, *outs)),
    )(left, a, b)


def contract_rows(left, right):
    return lax.dot_general(
        left, right, (((0,), (0,)), ((), ())), preferred_element_type=f32
    )


def swapped(values, axis, bit):
    size = lax.axis_size(axis)
    return lax.ppermute(values, axis, [(i, i ^ bit) for i in range(size)])


def shares(keeps, gives, axis, idle=0):
    came = [swapped(g, axis, 1) for g in gives]
    yield gives
    totals = [k + c.astype(f32) for k, c in zip(keeps, came)]
    bit = 2
    while bit < lax.axis_size(axis):
        sent = [t.astype(bf16) for t in totals]
        came = [swapped(v, axis, bit) for v in sent]
        yield sent
        for _ in range(idle):
            yield ()
        totals = [t + c.astype(f32) for t, c in zip(totals, came)]
        bit *= 2
    return totals


def both_shares(values, axis):
    odd = parity(axis) == 1
    came = [swapped(v, axis, 1) for v in values]
    yield values
    return [
        jnp.concatenate([jnp.where(odd, c, v), jnp.where(odd, v, c)], axis=1)
        for v, c in zip(values, came)
    ]


def line_cycles():
    size, cores = lax.axis_size("tp"), lax.axis_size("role")
    pairs = []
    for even in range(0, cores, 2):
        ring = [even * size + z for z in range(size)]
        ring += [(even + 1) * size + z for z in reversed(range(size))]
        pairs += [(ring[i - 1], ring[i]) for i in range(len(ring))]
    return pairs, [(b, a) for a, b in pairs]


def hop_body(plan, *refs):
    step, s, sums, out_sums, fresh_out, back, ready_in, came_in, counts, seen = plan
    chunks, parts, stripes, last = counts
    refs = list(refs)
    came = refs.pop(0) if came_in else None
    ready = refs.pop(0) if ready_in else None
    own = {}
    if sums:
        for q in seen:
            own[q] = (refs.pop(0), refs.pop(0))
    load = refs.pop(0)
    fresh = refs.pop(0) if fresh_out else None
    rows = load.shape[1]
    here, odd = lax.axis_index("tp"), parity("role")

    def place(stream):
        return jnp.where(odd == stream, here, last - here)

    if sums:
        group = chunks // (parts * stripes)
        index = jnp.clip(step - place(s), 0, chunks - 1)
        row = lax.div(index, group * stripes) * group + lax.rem(index, group)
        stripe = lax.rem(lax.div(index, group), stripes)
        cut = pl.ds(pl.multiple_of(row * rows, rows), rows)
        inner = place(s) > 0
        for q in seen:

            @pl.when(stripe == q)
            def _():
                pair = [ref[cut, :] for ref in own[q]]
                if step > 0:
                    pair = [
                        v + jnp.where(inner, came[i].astype(f32), 0.0)
                        for i, v in enumerate(pair)
                    ]
                if out_sums:
                    load[0] = pair[0].astype(bf16)
                    load[1] = pair[1].astype(bf16)
                if fresh_out:
                    fresh[...] = (jax.nn.silu(pair[0]) * pair[1]).astype(bf16)

    if back:
        slot, taken = load.shape[0] - 1, came.shape[0] - 1
        if ready_in and back == 1:
            load[slot] = ready[...]
        elif ready_in:
            ends = place(1 - s) == last

            @pl.when(ends)
            def _():
                load[slot] = ready[...]

            @pl.when(jnp.logical_not(ends))
            def _():
                load[slot] = came[taken]
        else:
            load[slot] = came[taken]


def tied(value, others):
    return lax.optimization_barrier((value, others))[0]


def teacher_hidden_parts(gate_up, stripes, positions, chunks, parts, beside):
    last = lax.axis_size("tp") - 1
    cycles = line_cycles()
    span = chunks // parts
    steps = chunks + 2 * last + 1
    held = ([], [])
    came = [None, None]
    fresh = [None, None]
    group = chunks // (parts * stripes)
    tokens, width = gate_up[0][0][0].shape
    rows = tokens * stripes // chunks
    for step in range(steps):
        sums = step <= chunks - 1 + last
        out_sums = step < chunks - 1 + last
        fresh_out = sums and step >= last
        sent = []
        made = [None, None]
        had = list(came)
        seen = sorted(
            {
                (c // group) % stripes
                for c in range(max(step - last, 0), min(step, chunks - 1) + 1)
            }
        )
        for s in (0, 1):
            r = 1 - s
            begin = last + r
            back = 0
            if begin <= step <= chunks - 1 + 2 * last + r:
                back = 1 if step == begin else 2
            ready = fresh[r] if back and step <= chunks - 1 + last + r else None
            depth = (2 if out_sums else 0) + (1 if back else 0)
            if not depth and not fresh_out:
                continue
            came_in = step > 0 and had[s] is not None
            operands = [had[s]] if came_in else []
            operands += [ready] if ready is not None else []
            if sums:
                operands += [gate_up[s][i][q] for q in seen for i in (0, 1)]
            outs = [jax.ShapeDtypeStruct((max(depth, 1), rows, width), bf16)]
            if fresh_out:
                outs.append(jax.ShapeDtypeStruct((rows, width), bf16))
            counts = (chunks, parts, stripes, last)
            plan = (
                step, s, sums, out_sums, fresh_out, back,
                ready is not None, came_in, counts, seen,
            )
            load, *rest = pl.pallas_call(
                functools.partial(hop_body, plan),
                in_specs=[VMEM] * len(operands),
                out_specs=[VMEM] * len(outs),
                out_shape=outs,
                compiler_params=pltpu.CompilerParams(vmem_limit_bytes=4 * MiB),
                cost_estimate=cost(rows * width * 8, nbytes(*outs) * 2),
            )(*operands)
            if fresh_out:
                made[s] = rest[0]
                if s == 0:
                    fresh[0] = rest[0]
            if back:
                held[r].append(load[depth - 1])
            if out_sums or (back and step < chunks - 1 + 2 * last + r):
                came[s] = lax.ppermute(load, ("role", "tp"), cycles[s])
                sent.append(load)
            else:
                came[s] = None
        fresh[1] = made[1]
        if made[0] is None:
            fresh[0] = None
        for part in range(parts):
            if step - last == (part + 1) * span + last:
                sides = []
                for s in (0, 1):
                    seen = jnp.stack(held[s][part * span : (part + 1) * span + last])
                    mine = lax.dynamic_slice_in_dim(seen, last - positions[s], span, 0)
                    sides.append(mine.reshape(stripes, -1, mine.shape[-1]))
                yield part, jnp.concatenate(sides)
        after = beside(step, sent)
        if after is not None and step < steps - 1:
            came = [None if c is None else tied(c, after) for c in came]


def on_device(x_teacher, x_student, t_gate, t_up, t_down, s_gate, s_up, s_down, align):
    tokens = x_teacher.shape[0]
    half = t_gate.shape[1] // 2
    parts, chunks = 2, 8
    rows = tokens // parts
    stripes = 2 if half % 256 == 0 else 1
    last = lax.axis_size("tp") - 1
    here = lax.axis_index("tp")
    odd = parity("role")
    positions = [jnp.where(odd == s, here, last - here) for s in (0, 1)]

    def teacher_terms(q, x):
        def side(s, core):
            return ((1 - core) if s == 0 else core) * stripes + q

        jobs = [
            (w, functools.partial(side, s), f32) for s in (0, 1) for w in (0, 1)
        ]
        return terms(x, (t_gate, t_up), half // stripes, jobs)

    gate_up = [[[], []], [[], []]]

    def add_terms(q, x):
        found = teacher_terms(q, x)
        for s in (0, 1):
            for i in (0, 1):
                gate_up[s][i].append(found[2 * s + i])
        return found

    saved = {}

    def student(x):
        jobs = [(w, lambda core: 1 - core, bf16) for w in (0, 1)]
        jobs += [(w, lambda core: core, f32) for w in (0, 1)]
        found = terms(x, (s_gate, s_up), s_gate.shape[1] // 2, jobs)
        gate, up = yield from shares(found[2:], found[:2], "role", 2)
        sigmoid = jax.nn.sigmoid(gate)
        active = gate * sigmoid
        (hidden,) = yield from both_shares([(active * up).astype(bf16)], "role")
        keep, give = halves("tp", NN, hidden, s_down)
        (share,) = yield from shares([keep], [give], "tp")
        (out,) = yield from both_shares([share.astype(bf16)], "tp")
        saved.update(
            gate=gate, up=up, sigmoid=sigmoid, active=active, hidden=hidden, out=out
        )
        saved["turned"] = turned(x_student)
        yield [out]

    running = []

    def beside(step, sent):
        if step < 2 and len(gate_up[0][0]) < stripes:
            return add_terms(len(gate_up[0][0]), tied(x_teacher, sent))
        if step == 2:
            running.append(student(tied(x_student, sent)))
        if running:
            done = next(running[0], None)
            if done is None:
                running.clear()
            return done
        return None

    add_terms(0, x_teacher)
    results = []

    def tail(part, hidden):
        cut = slice(part * rows, (part + 1) * rows)
        gate, up, sigmoid, active = [
            saved[k][cut] for k in ("gate", "up", "sigmoid", "active")
        ]
        out = saved["out"][cut]
        keep, give = difference_terms(stripes, hidden, out, t_down, align)
        (difference,) = yield from shares([keep], [give], "role")
        scaled = (difference * (2.0 * loss_scale / tokens)).astype(bf16)
        (grad_aligned,) = yield from both_shares([scaled], "role")
        keep, give = halves("tp", NT, grad_aligned, align)
        (share,) = yield from shares([keep], [give], "tp")
        (grad_out,) = yield from both_shares([share.astype(bf16)], "tp")
        keep, give = halves("role", NT, grad_out, s_down)
        (grad_hidden,) = yield from shares([keep], [give], "role")
        slope = sigmoid * (1.0 + gate * (1.0 - sigmoid))
        grads = [
            (grad_hidden * up * slope).astype(bf16),
            (grad_hidden * active).astype(bf16),
        ]
        pres = yield from both_shares(grads, "role")
        results.append((grad_aligned, grad_out, *pres))

    waiting = list(teacher_hidden_parts(gate_up, stripes, positions, chunks, parts, beside))
    while running:
        beside(chunks + 2 * last + 1, [])
    for part, hidden in waiting:
        for _ in tail(part, hidden):
            pass
    grad_aligned, grad_out, gate_pre, up_pre = [
        jnp.concatenate([r[i] for r in results], axis=0) for i in range(4)
    ]
    grad_align = contract_rows(saved["out"], grad_aligned).astype(bf16)
    grad_s_down = contract_rows(saved["hidden"], grad_out).astype(bf16)
    grad_s_gate, grad_s_up = outer_pair(saved["turned"], gate_pre, up_pre)
    return (grad_s_gate, grad_s_up, grad_s_down, grad_align)


def solution(mesh):
    placed = (
        P("groups", "tp"),
        P("groups", "role"),
        P("tp", "role"),
        P("tp", "role"),
        P("role", "tp"),
        P("role", "tp"),
        P("role", "tp"),
        P("tp", "role"),
        P("role", "tp"),
    )
    return jax.shard_map(
        on_device,
        mesh=mesh,
        in_specs=placed,
        out_specs=(
            P(("groups", "role"), "tp"),
            P(("groups", "role"), "tp"),
            P(("groups", "tp"), "role"),
            P(("groups", "role"), "tp"),
        ),
        check_vma=False,
    )
```

```python
import functools

import jax
import jax.numpy as jnp
from jax import lax
from jax.experimental import pallas as pl
from jax.experimental.pallas import tpu as pltpu
from jax.sharding import PartitionSpec as P

loss_scale = 16.0
f32 = jnp.float32
bf16 = jnp.bfloat16
MiB = 1 << 20


HBM = pl.BlockSpec(memory_space=pltpu.HBM)
VMEM = pl.BlockSpec(memory_space=pltpu.VMEM)
NN = (((1,), (0,)), ((), ()))
NT = (((1,), (1,)), ((), ()))


def parity(axis):
    return lax.rem(lax.axis_index(axis), 2)


def cost(flops, moved):
    return pl.CostEstimate(flops=flops, bytes_accessed=moved, transcendentals=0)


def nbytes(*arrays):
    return sum(a.size * a.dtype.itemsize for a in arrays)


def terms_body(jobs, pieces, x_ref, *refs):
    weights, refs = refs[: len(jobs[0][0])], refs[len(jobs[0][0]) :]
    outs, (x_buf, w_buf, x_sem, w_sem) = refs[: len(jobs)], refs[len(jobs) :]
    deep, width = w_buf.shape[2:]
    odd = parity("role")

    def x_copy(i):
        return pltpu.make_async_copy(
            x_ref.at[:, pl.ds(i * deep, deep)], x_buf.at[i], x_sem.at[i]
        )

    def w_copy(j, i):
        which, side_of = jobs[j][1:3]
        side = pl.multiple_of(side_of(odd) * width, 128)
        return pltpu.make_async_copy(
            weights[which].at[pl.ds(i * deep, deep), pl.ds(side, width)],
            w_buf.at[j, i],
            w_sem.at[j, i],
        )

    for j in range(len(jobs)):
        for i in range(pieces):
            if j == 0:
                x_copy(i).start()
            w_copy(j, i).start()
    for j in range(len(jobs)):
        total = None
        for i in range(pieces):
            if j == 0:
                x_copy(i).wait()
            w_copy(j, i).wait()
            term = jnp.dot(x_buf[i], w_buf[j, i], preferred_element_type=f32)
            total = term if total is None else total + term
        outs[j][...] = total.astype(outs[j].dtype)


def terms(x, weights, width, jobs, grant):
    rows, depth = x.shape
    if width % 128:
        odd = parity("role")
        cut = [
            lax.dynamic_slice_in_dim(weights[w], side(odd) * width, width, 1)
            for w, side, _ in jobs
        ]
        return [
            jnp.dot(x, c, preferred_element_type=f32).astype(j[2])
            for c, j in zip(cut, jobs)
        ]
    pieces = 4 if depth % 1024 == 0 else 1
    deep = depth // pieces
    named = [(weights, *job) for job in jobs]
    outs = [jax.ShapeDtypeStruct((rows, width), j[2]) for j in jobs]
    return pl.pallas_call(
        functools.partial(terms_body, named, pieces),
        in_specs=[HBM] * (1 + len(weights)),
        out_specs=[VMEM] * len(jobs),
        out_shape=outs,
        scratch_shapes=[
            pltpu.VMEM((pieces, rows, deep), bf16),
            pltpu.VMEM((len(jobs), pieces, deep, width), bf16),
            pltpu.SemaphoreType.DMA((pieces,)),
            pltpu.SemaphoreType.DMA((len(jobs), pieces)),
        ],
        compiler_params=pltpu.CompilerParams(vmem_limit_bytes=grant * MiB),
        cost_estimate=cost(
            2 * len(jobs) * rows * depth * width,
            2 * len(jobs) * depth * width + nbytes(x, *outs),
        ),
    )(x, *weights)


def halves_body(axis, dims, left_ref, right_ref, keep_ref, give_ref):
    odd = parity(axis)
    width = keep_ref.shape[1]
    left = left_ref[...]
    for out, side in ((give_ref, 1 - odd), (keep_ref, odd)):
        cut = pl.ds(pl.multiple_of(side * width, 128), width)
        right = right_ref[:, cut] if dims == NN else right_ref[cut, :]
        term = lax.dot_general(left, right, dims, preferred_element_type=f32)
        out[...] = term.astype(out.dtype)


def halves(axis, dims, left, right):
    rows = left.shape[0]
    width = (right.shape[1] if dims == NN else right.shape[0]) // 2
    outs = [
        jax.ShapeDtypeStruct((rows, width), f32),
        jax.ShapeDtypeStruct((rows, width), bf16),
    ]
    return pl.pallas_call(
        functools.partial(halves_body, axis, dims),
        in_specs=[VMEM] * 2,
        out_specs=[VMEM] * 2,
        out_shape=outs,
        compiler_params=pltpu.CompilerParams(vmem_limit_bytes=16 * MiB),
        cost_estimate=cost(
            2 * left.shape[0] * right.size, nbytes(left, right, *outs)
        ),
    )(left, right)


def difference_body(stripes, hidden_ref, out_ref, down_ref, align_ref, keep_ref, give_ref):
    odd = parity("role")
    width = keep_ref.shape[1]
    tile = 256 if width % 256 == 0 else width
    depth = hidden_ref.shape[2]
    for result, side in ((give_ref, 1 - odd), (keep_ref, odd)):
        for first in range(0, width, tile):
            cut = pl.ds(pl.multiple_of(side * width + first, 128), tile)
            total = jnp.dot(out_ref[...], align_ref[:, cut], preferred_element_type=f32)
            for s in (0, 1):
                upward = 1 - odd if s == 0 else odd
                for q in range(stripes):
                    row = pl.multiple_of((upward * stripes + q) * depth, 64)
                    total -= jnp.dot(
                        hidden_ref[s * stripes + q],
                        down_ref[pl.ds(row, depth), cut],
                        preferred_element_type=f32,
                    )
            result[:, first : first + tile] = total.astype(result.dtype)


def difference_terms(stripes, hidden, out, down, align):
    rows, width = out.shape[0], down.shape[1] // 2
    outs = [
        jax.ShapeDtypeStruct((rows, width), f32),
        jax.ShapeDtypeStruct((rows, width), bf16),
    ]
    return pl.pallas_call(
        functools.partial(difference_body, stripes),
        in_specs=[VMEM] * 4,
        out_specs=[VMEM] * 2,
        out_shape=outs,
        compiler_params=pltpu.CompilerParams(vmem_limit_bytes=30 * MiB),
        cost_estimate=cost(
            2 * rows * (down.size + align.size),
            nbytes(hidden, out, down, align, *outs),
        ),
    )(hidden, out, down, align)


def turned_body(x_ref, o_ref):
    o_ref[...] = x_ref[...].T


def turned(x):
    return pl.pallas_call(
        turned_body,
        in_specs=[VMEM],
        out_specs=VMEM,
        out_shape=jax.ShapeDtypeStruct(x.shape[::-1], x.dtype),
        compiler_params=pltpu.CompilerParams(vmem_limit_bytes=8 * MiB),
        cost_estimate=cost(0, 2 * nbytes(x)),
    )(x)


def outer_body(left_ref, a_ref, b_ref, oa_ref, ob_ref):
    left = left_ref[...]
    oa_ref[...] = jnp.dot(left, a_ref[...], preferred_element_type=f32).astype(bf16)
    ob_ref[...] = jnp.dot(left, b_ref[...], preferred_element_type=f32).astype(bf16)


def outer_pair(left, a, b):
    rows, tokens = left.shape
    width = a.shape[1]
    block = 128 if rows % 128 == 0 else rows
    right = pl.BlockSpec((tokens, width), lambda j: (0, 0))
    result = pl.BlockSpec((block, width), lambda j: (j, 0))
    outs = [jax.ShapeDtypeStruct((rows, width), bf16)] * 2
    return pl.pallas_call(
        outer_body,
        grid=(rows // block,),
        in_specs=[pl.BlockSpec((block, tokens), lambda j: (j, 0)), right, right],
        out_specs=[result, result],
        out_shape=outs,
        compiler_params=pltpu.CompilerParams(vmem_limit_bytes=24 * MiB),
        cost_estimate=cost(4 * rows * tokens * width, nbytes(left, a, b, *outs)),
    )(left, a, b)


def contract_rows(left, right):
    return lax.dot_general(
        left, right, (((0,), (0,)), ((), ())), preferred_element_type=f32
    )


def swapped(values, axis, bit):
    size = lax.axis_size(axis)
    return lax.ppermute(values, axis, [(i, i ^ bit) for i in range(size)])


def tied(value, others):
    return lax.optimization_barrier((value, others))[0]


def shares(keeps, gives, axis):
    came = [swapped(g, axis, 1) for g in gives]
    after = (yield gives) if axis == "tp" else None
    bit = 2
    totals = keeps
    while True:
        if after:
            came = tied(came, after)
        totals = [t + c.astype(f32) for t, c in zip(totals, came)]
        if bit >= lax.axis_size(axis):
            return totals
        sent = [t.astype(bf16) for t in totals]
        came = [swapped(v, axis, bit) for v in sent]
        after = yield sent
        bit *= 2


def both_shares(values, axis):
    odd = parity(axis) == 1
    came = [swapped(v, axis, 1) for v in values]
    after = (yield values) if axis == "tp" else None
    if after:
        came = tied(came, after)
    return [
        jnp.concatenate([jnp.where(odd, c, v), jnp.where(odd, v, c)], axis=1)
        for v, c in zip(values, came)
    ]


def line_cycles():
    size, cores = lax.axis_size("tp"), lax.axis_size("role")
    pairs = []
    for even in range(0, cores, 2):
        ring = [even * size + z for z in range(size)]
        ring += [(even + 1) * size + z for z in reversed(range(size))]
        pairs += [(ring[i - 1], ring[i]) for i in range(len(ring))]
    return pairs, [(b, a) for a, b in pairs]


def hop_body(plan, *refs):
    step, s, sums, out_sums, fresh_out, back, ready_in, came_in, counts, seen = plan
    chunks, parts, stripes, last = counts
    refs = list(refs)
    came = refs.pop(0) if came_in else None
    ready = refs.pop(0) if ready_in else None
    own = {}
    if sums:
        for q in seen:
            own[q] = (refs.pop(0), refs.pop(0))
    load = refs.pop(0)
    fresh = refs.pop(0) if fresh_out else None
    rows = load.shape[1]
    here, odd = lax.axis_index("tp"), parity("role")

    def place(stream):
        return jnp.where(odd == stream, here, last - here)

    if sums:
        group = chunks // (parts * stripes)
        index = jnp.clip(step - place(s), 0, chunks - 1)
        row = lax.div(index, group * stripes) * group + lax.rem(index, group)
        stripe = lax.rem(lax.div(index, group), stripes)
        cut = pl.ds(pl.multiple_of(row * rows, rows), rows)
        inner = place(s) > 0
        for q in seen:

            @pl.when(stripe == q)
            def _():
                pair = [ref[cut, :] for ref in own[q]]
                if step > 0:
                    pair = [
                        v + jnp.where(inner, came[i].astype(f32), 0.0)
                        for i, v in enumerate(pair)
                    ]
                if out_sums:
                    load[0] = pair[0].astype(bf16)
                    load[1] = pair[1].astype(bf16)
                if fresh_out:
                    fresh[...] = (jax.nn.silu(pair[0]) * pair[1]).astype(bf16)

    if back:
        slot, taken = load.shape[0] - 1, came.shape[0] - 1
        if ready_in and back == 1:
            load[slot] = ready[...]
        elif ready_in:
            ends = place(1 - s) == last

            @pl.when(ends)
            def _():
                load[slot] = ready[...]

            @pl.when(jnp.logical_not(ends))
            def _():
                load[slot] = came[taken]
        else:
            load[slot] = came[taken]


def teacher_hidden_parts(gate_up, stripes, positions, chunks, parts, beside):
    last = lax.axis_size("tp") - 1
    cycles = line_cycles()
    span = chunks // parts
    steps = chunks + 2 * last + 1
    held = ([], [])
    came = [None, None]
    fresh = [None, None]
    group = chunks // (parts * stripes)
    tokens, width = gate_up[0][0][0].shape
    rows = tokens * stripes // chunks
    for step in range(steps):
        sums = step <= chunks - 1 + last
        out_sums = step < chunks - 1 + last
        fresh_out = sums and step >= last
        sent = []
        made = [None, None]
        had = list(came)
        seen = sorted(
            {
                (c // group) % stripes
                for c in range(max(step - last, 0), min(step, chunks - 1) + 1)
            }
        )
        for s in (0, 1):
            r = 1 - s
            begin = last + r
            back = 0
            if begin <= step <= chunks - 1 + 2 * last + r:
                back = 1 if step == begin else 2
            ready = fresh[r] if back and step <= chunks - 1 + last + r else None
            depth = (2 if out_sums else 0) + (1 if back else 0)
            if not depth and not fresh_out:
                continue
            came_in = step > 0 and had[s] is not None
            operands = [had[s]] if came_in else []
            operands += [ready] if ready is not None else []
            if sums:
                operands += [gate_up[s][i][q] for q in seen for i in (0, 1)]
            outs = [jax.ShapeDtypeStruct((max(depth, 1), rows, width), bf16)]
            if fresh_out:
                outs.append(jax.ShapeDtypeStruct((rows, width), bf16))
            counts = (chunks, parts, stripes, last)
            plan = (
                step, s, sums, out_sums, fresh_out, back,
                ready is not None, came_in, counts, seen,
            )
            load, *rest = pl.pallas_call(
                functools.partial(hop_body, plan),
                in_specs=[VMEM] * len(operands),
                out_specs=[VMEM] * len(outs),
                out_shape=outs,
                compiler_params=pltpu.CompilerParams(vmem_limit_bytes=4 * MiB),
                cost_estimate=cost(rows * width * 8, nbytes(*outs) * 2),
            )(*operands)
            if fresh_out:
                made[s] = rest[0]
                if s == 0:
                    fresh[0] = rest[0]
            if back:
                held[r].append(load[depth - 1])
            if out_sums or (back and step < chunks - 1 + 2 * last + r):
                came[s] = lax.ppermute(load, ("role", "tp"), cycles[s])
                sent.append(load)
            else:
                came[s] = None
        fresh[1] = made[1]
        if made[0] is None:
            fresh[0] = None
        for part in range(parts):
            if step - last == (part + 1) * span + last:
                sides = []
                for s in (0, 1):
                    seen = jnp.stack(held[s][part * span : (part + 1) * span + last])
                    mine = lax.dynamic_slice_in_dim(seen, last - positions[s], span, 0)
                    sides.append(mine.reshape(stripes, -1, mine.shape[-1]))
                yield part, jnp.concatenate(sides)
        after = beside(step, sent)
        if after is not None and step < steps - 1:
            came = [None if c is None else tied(c, after) for c in came]


def on_device(x_teacher, x_student, t_gate, t_up, t_down, s_gate, s_up, s_down, align):
    tokens = x_teacher.shape[0]
    half = t_gate.shape[1] // 2
    parts, chunks = 2, 8
    rows = tokens // parts
    stripes = 2 if half % 256 == 0 else 1
    last = lax.axis_size("tp") - 1
    here = lax.axis_index("tp")
    odd = parity("role")
    positions = [jnp.where(odd == s, here, last - here) for s in (0, 1)]

    def teacher_terms(q, x):
        def side(s, core):
            return ((1 - core) if s == 0 else core) * stripes + q

        jobs = [
            (w, functools.partial(side, s), f32) for s in (0, 1) for w in (0, 1)
        ]
        return terms(x, (t_gate, t_up), half // stripes, jobs, 47)

    gate_up = [[[], []], [[], []]]

    def add_terms(q, x):
        found = teacher_terms(q, x)
        for s in (0, 1):
            for i in (0, 1):
                gate_up[s][i].append(found[2 * s + i])
        return found

    saved = {}

    def student(x):
        jobs = [(w, lambda core: 1 - core, bf16) for w in (0, 1)]
        jobs += [(w, lambda core: core, f32) for w in (0, 1)]
        found = terms(x, (s_gate, s_up), s_gate.shape[1] // 2, jobs, 52)
        gate, up = yield from shares(found[2:], found[:2], "role")
        sigmoid = jax.nn.sigmoid(gate)
        active = gate * sigmoid
        (hidden,) = yield from both_shares([(active * up).astype(bf16)], "role")
        keep, give = halves("tp", NN, hidden, s_down)
        (share,) = yield from shares([keep], [give], "tp")
        (out,) = yield from both_shares([share.astype(bf16)], "tp")
        saved.update(
            gate=gate, up=up, sigmoid=sigmoid, active=active, hidden=hidden, out=out
        )
        saved["turned"] = turned(x_student)

    def advance(work, after=None):
        try:
            return work.send(after)
        except StopIteration:
            return ()

    results = [None] * parts

    def tail(part, hidden):
        cut = slice(part * rows, (part + 1) * rows)
        gate, up, sigmoid, active = [
            saved[k][cut] for k in ("gate", "up", "sigmoid", "active")
        ]
        out = saved["out"][cut]
        keep, give = difference_terms(stripes, hidden, out, t_down, align)
        (difference,) = yield from shares([keep], [give], "role")
        scaled = (difference * (2.0 * loss_scale / tokens)).astype(bf16)
        (grad_aligned,) = yield from both_shares([scaled], "role")
        keep, give = halves("tp", NT, grad_aligned, align)
        results[part] = [grad_aligned]
        (share,) = yield from shares([keep], [give], "tp")
        (grad_out,) = yield from both_shares([share.astype(bf16)], "tp")
        results[part].append(grad_out)
        keep, give = halves("role", NT, grad_out, s_down)
        (grad_hidden,) = yield from shares([keep], [give], "role")
        slope = sigmoid * (1.0 + gate * (1.0 - sigmoid))
        grads = [
            (grad_hidden * up * slope).astype(bf16),
            (grad_hidden * active).astype(bf16),
        ]
        results[part] += yield from both_shares(grads, "role")

    student_work = []
    tails = []

    def beside(step, sent):
        if step == 0:
            student_work.append(student(tied(x_student, sent)))
            return advance(student_work[0])
        if step == 1 and stripes > 1:
            return add_terms(1, tied(x_teacher, sent))
        if step >= 3 and "out" not in saved:
            return advance(student_work[0], sent)
        if tails:
            age = step - tails[0][1]
            if age == 0:
                return advance(tails[0][0])
            if age > 1:
                return advance(tails[0][0], sent)
        return None

    add_terms(0, x_teacher)
    for part, hidden in teacher_hidden_parts(
        gate_up, stripes, positions, chunks, parts, beside
    ):
        if part == 0:
            while "out" not in saved:
                advance(student_work[0])
        tails.append((tail(part, hidden), 2 * last + (part + 1) * chunks // parts + 1))

    def drain(work):
        while advance(work) != ():
            pass

    def joined(i):
        return jnp.concatenate([r[i] for r in results], axis=0)

    for work, _ in tails[:-1]:
        drain(work)
    work = tails[-1][0]
    final = []
    sent = advance(work)
    while sent != ():
        after = None
        if results[-1] and len(results[-1]) == 1 and not final:
            final.append(
                contract_rows(tied(saved["out"], sent), joined(0)).astype(bf16)
            )
            after = final[-1:]
        elif results[-1] and len(results[-1]) == 2 and len(final) == 1:
            final.append(
                contract_rows(tied(saved["hidden"], sent), joined(1)).astype(bf16)
            )
            after = final[-1:]
        sent = advance(work, after)
    grad_align, grad_s_down = final
    grad_s_gate, grad_s_up = outer_pair(saved["turned"], joined(2), joined(3))
    return (grad_s_gate, grad_s_up, grad_s_down, grad_align)


def solution(mesh):
    placed = (
        P("groups", "tp"),
        P("groups", "role"),
        P("tp", "role"),
        P("tp", "role"),
        P("role", "tp"),
        P("role", "tp"),
        P("role", "tp"),
        P("tp", "role"),
        P("role", "tp"),
    )
    return jax.shard_map(
        on_device,
        mesh=mesh,
        in_specs=placed,
        out_specs=(
            P(("groups", "role"), "tp"),
            P(("groups", "role"), "tp"),
            P(("groups", "tp"), "role"),
            P(("groups", "role"), "tp"),
        ),
        check_vma=False,
    )
```
